256 devices in a mesh: row: 4 (over y), col: 64 (over x, z, core).
Axes of the slice: x: 4, y: 4, z: 8, core: 2. Of those that a mesh axis runs over, the one named last changes fastest.
Arguments:
- a_tiles: bfloat16 [256, 8, 128, 128], P(('row', 'col')), may hold values from 0.0099487305 to 1
- b_tiles: bfloat16 [4, 4096, 128, 128], P('row', 'col'), may hold values from 0.0099487305 to 1
- b_block: int32 [4, 4096], P('row', 'col'), may hold values from 0 to 63
- c_slot: int32 [4, 4096, 8], P('row', 'col'), may hold values from 0 to 127, as said below
- b_live: int32 [4, 64], P('row', 'col'), may hold values from 16 to 64, as said below
Outputs:
- inflated: bfloat16 [128, 64, 128, 128], P('row', 'col')
The draws below stay inside these ranges and needn't reach their ends.
Inputs may be any that keep to these rules, and one draw needn't show every extreme that they name: c_slot mod 8 is the block column of the product; it is the same for all 8 products of one slot, and every block column occurs among the first 8 slots of each device. `b_live`: some device has exactly 64 live slots and some device exactly 16.
All inputs are finite; a program needn't handle non-finite values.
Results may differ from the reference program's by a relative error of at most 0.022.
Values may be sent and summed in bfloat16 or wider, within the bound.
No kernel may reach another device: no remote copies, remote signals or barrier semaphores. Data moves between devices by JAX's collectives and lax.ppermute only.
A program may use at most 192 MiB of HBM per device.

```python
import math
import jax
import jax.numpy as jnp
from jax import lax

TILE = 128
NNZ = 8
K_DEV = 1
JB_DEV = 8
OUT_J = 16
TB = 64
KR = 64
KW = 256
N_ROW = 4
N_COL = 64


def draw_c_slot(key, part):
    key_column_position = jax.random.fold_in(key, 11)
    key_off = jax.random.fold_in(key, 12)
    key_in = jax.random.fold_in(key, 13)
    device_rows = N_ROW * N_COL
    column = jax.random.randint(key_column_position, (device_rows, TB), 0, JB_DEV)
    offset = jax.random.randint(key_off, (device_rows, 1), 0, JB_DEV)
    positions = jnp.arange(TB, dtype=jnp.int32)[None, :]
    leading = (positions + offset) % JB_DEV
    column = jnp.where(positions < JB_DEV, leading, column)
    within = jax.random.randint(key_in, (device_rows, TB, NNZ), 0, OUT_J)
    slot_numbers = within * JB_DEV + column[:, :, None]
    return slot_numbers.reshape(N_ROW, N_COL * TB, NNZ).astype(jnp.int32)


def draw_b_live(key, part):
    key_count = jax.random.fold_in(key, 21)
    key_full = jax.random.fold_in(key, 22)
    key_least = jax.random.fold_in(key, 23)
    processor_total = N_ROW * N_COL
    entry_tallies = jax.random.randint(key_count, (processor_total,), TB // 4, TB + 1)
    full_pick = jax.random.randint(key_full, (), 0, processor_total)
    least_pick = (full_pick + 1 + jax.random.randint(key_least, (), 0, processor_total - 1)) % processor_total
    places = jnp.arange(processor_total, dtype=jnp.int32)
    entry_tallies = jnp.where(places == full_pick, TB, entry_tallies)
    entry_tallies = jnp.where(places == least_pick, TB // 4, entry_tallies)
    return entry_tallies.reshape(N_ROW, N_COL).astype(jnp.int32)


def plant(values, stream_key, least, largest):
    longest = values.shape.index(max(values.shape))
    spots = []
    for shift in (0, 1):
        where = [jax.random.randint(jax.random.fold_in(stream_key, axis), (), 0, length) for axis, length in enumerate(values.shape)]
        where[longest] = (where[longest] + shift) % values.shape[longest]
        spots.append(tuple(where))
    return values.at[spots[0]].set(least).at[spots[1]].set(largest)


def levels(own_key, dims, pieces, least, largest):
    level = 1.0
    for axis_at, blocks in pieces:
        draws = jax.random.uniform(jax.random.fold_in(jax.random.fold_in(own_key, 6), axis_at), (blocks,), jnp.float32, least / len(pieces), largest / len(pieces))
        level = level * jnp.repeat(jnp.exp(draws), dims[axis_at] // blocks).reshape((-1,) + (1,) * (len(dims) - 1 - axis_at))
    return level


def setup_inputs(seed: int = 0) -> dict:
    seeds = jax.random.split(jax.random.key(seed), 6)
    a_tiles = jnp.clip(jnp.exp(math.log(1.0) - 4.61031033 * jax.random.uniform(seeds[0], (KW, NNZ, TILE, TILE), jnp.float32) ** levels(seeds[0], (KW, NNZ, TILE, TILE), ((0, 256),), -0.2, 0.2)), 0.0099487305, 1.0).astype(jnp.bfloat16)
    b_tiles = jnp.clip(jnp.exp(math.log(1.0) - 4.61031033 * jax.random.uniform(seeds[1], (N_ROW, N_COL * TB, TILE, TILE), jnp.float32) ** levels(seeds[1], (N_ROW, N_COL * TB, TILE, TILE), ((0, 4), (1, 64)), -0.2, 0.2)), 0.0099487305, 1.0).astype(jnp.bfloat16)
    b_block = plant(jax.random.randint(seeds[2], (N_ROW, N_COL * TB), 0, KR), jax.random.fold_in(seeds[2], 1), 0, KR - 1).astype(jnp.int32)
    c_slot = draw_c_slot(jax.random.fold_in(seeds[5], 71), 0)
    b_live = draw_b_live(jax.random.fold_in(seeds[5], 71), 0)
    return dict(a_tiles=a_tiles, b_tiles=b_tiles, b_block=b_block, c_slot=c_slot, b_live=b_live)


def apply_inflation_power(reduced_totals):
    slot_count = reduced_totals.shape[0]
    squared = reduced_totals * reduced_totals
    owner_col = jnp.arange(slot_count, dtype=jnp.int32) % JB_DEV
    onehot = (owner_col[:, None] == jnp.arange(JB_DEV, dtype=jnp.int32)[None, :]).astype(squared.dtype)
    column_total = jnp.dot(onehot.T, jnp.sum(squared, axis=1), precision=lax.Precision.HIGHEST)
    factor = (OUT_J * TILE) / jnp.dot(onehot, column_total, precision=lax.Precision.HIGHEST)
    return (squared * factor[:, None, :]).astype(jnp.bfloat16)


def reference(a_tiles, b_tiles, b_block, c_slot, b_live):
    group_blocks = K_DEV * N_COL
    slot_count = OUT_J * JB_DEV

    def panel(column):
        reduced_totals = jnp.zeros((slot_count, TILE, TILE), jnp.float32)
        for row_index in range(N_ROW):
            b_panel = lax.dynamic_slice_in_dim(b_tiles[row_index], column * TB, TB, 0)
            blocks = lax.dynamic_slice_in_dim(b_block[row_index], column * TB, TB, 0)
            slot_numbers = lax.dynamic_slice_in_dim(c_slot[row_index], column * TB, TB, 0)
            chosen = jnp.take(a_tiles, blocks + row_index * group_blocks, axis=0).astype(jnp.float32)
            product = jnp.einsum("tmab,tbc->tmac", chosen, b_panel.astype(jnp.float32))
            is_live = jnp.arange(TB, dtype=jnp.int32) < b_live[row_index, column]
            product = jnp.where(is_live[:, None, None, None], product, 0.0)
            partial_value = jax.ops.segment_sum(product.reshape(TB * NNZ, TILE, TILE), slot_numbers.reshape(TB * NNZ), num_segments=slot_count)
            reduced_totals = reduced_totals + partial_value.astype(jnp.bfloat16).astype(jnp.float32)
        return apply_inflation_power(reduced_totals)

    final_matrix = lax.map(panel, jnp.arange(N_COL, dtype=jnp.int32))
    return jnp.transpose(final_matrix, (1, 0, 2, 3))
```

```python
import functools

import jax
import jax.numpy as jnp
from jax import lax
from jax.experimental import pallas as pl
from jax.experimental.pallas import tpu as pltpu
from jax.sharding import Mesh
from jax.sharding import PartitionSpec as P

JB_DEV = 8
OUT_J = 16
TILE = 128
NNZ = 8
TB = 64
SLOTS = 128
NX, NY, NZ = 4, 4, 8
SIZES = {"y": NY, "x": NX, "z": NZ, "c": 2}
ROWS = TILE // 2
FIRST = 32
VMEM_LIMIT = 60 * 1024 * 1024


def shift(value, axis, step):
    n = SIZES[axis]
    return lax.ppermute(value, axis, [(i, (i + step) % n) for i in range(n)])


def ring_place(distance, n):
    return jnp.maximum(jnp.minimum(2 * distance - 1, 2 * (n - distance)), 0)


def gather_left(first, second):
    x_behind, x_ahead, x_far = shift(first, "x", 1), shift(first, "x", -1), shift(first, "x", 2)
    z1, w1 = shift(second, "z", 1), shift(second, "z", -1)
    own = jnp.concatenate([first, x_behind, x_ahead, x_far])
    b1, a1 = shift(own, "z", 1), shift(own, "z", -1)
    z2, w2 = shift(z1, "z", 1), shift(w1, "z", -1)
    b2, a2 = shift(b1, "z", 1), shift(a1, "z", -1)
    z3, w3 = shift(z2, "z", 1), shift(w2, "z", -1)
    z4 = shift(z3, "z", 1)
    column = jnp.concatenate([second, z1, w1, z2, w2, z3, w3, z4])
    r, l = shift(column, "x", 1), shift(column, "x", -1)
    b3, a3 = shift(b2, "z", 1), shift(a2, "z", -1)
    half = own.shape[0] // 2
    b4, a4 = shift(b3[:half], "z", 1), shift(a3[half:], "z", -1)
    half = column.shape[0] // 2
    r2, l2 = shift(r[:half], "x", 1), shift(l[half:], "x", -1)
    return [own, b1, a1, b2, a2, b3, a3, b4, a4], [column, r, l, r2, l2]


def expand_kernel(rows, n_pieces, place, slot, live, me, *refs):
    pieces = refs[:n_pieces]
    b_own, b_sib, out = refs[n_pieces : n_pieces + 3]
    left, right, acc0, acc1, rounded, sems, out_sems = refs[n_pieces + 3 :]
    copies, at = [], 0
    for n, piece in enumerate(pieces):
        count = piece.shape[0]
        copies.append(pltpu.make_async_copy(piece, left.at[pl.ds(at, count)], sems.at[n]))
        at += count
    copies.append(pltpu.make_async_copy(b_own, right.at[0], sems.at[n_pieces]))
    copies.append(pltpu.make_async_copy(b_sib, right.at[1], sems.at[n_pieces + 1]))
    for copy in copies:
        copy.start()

    def clear(i, carry):
        acc0[i] = jnp.zeros((rows, TILE), jnp.float32)
        acc1[i] = jnp.zeros((rows, TILE), jnp.float32)
        return carry

    lax.fori_loop(0, SLOTS, clear, 0, unroll=8)
    for copy in copies:
        copy.wait()

    def step(t, carry):
        both = jnp.concatenate([left[place[t]], left[place[TB + t]]], axis=1)
        zero = jnp.zeros((TILE, TILE), jnp.bfloat16)
        own = jnp.where(t < live[0], right[0, t], zero)
        sib = jnp.where(t < live[1], right[1, t], zero)
        weights = jnp.concatenate(
            [jnp.concatenate([own, zero], axis=1), jnp.concatenate([zero, sib], axis=1)], axis=0
        )
        product = jnp.dot(both, weights, preferred_element_type=jnp.float32)
        for m in range(NNZ):
            part = product[m * rows : (m + 1) * rows]
            acc0[slot[t * NNZ + m]] += part[:, :TILE]
            acc1[slot[(TB + t) * NNZ + m]] += part[:, TILE:]
        return carry

    lax.fori_loop(0, jnp.maximum(live[0], live[1]), step, 0)
    share = SLOTS // NY
    copies = []
    for q, acc in ((0, acc0), (1, acc1)):
        for y in range(NY):

            def narrow(i, carry, q=q, y=y, acc=acc):
                rounded[q, y, i] = acc[y * share + i].astype(jnp.bfloat16)
                return carry

            lax.fori_loop(0, share, narrow, 0, unroll=8)
            copy = pltpu.make_async_copy(
                rounded.at[q, y], out.at[2 * y + jnp.bitwise_xor(me[0], q)], out_sems.at[q, y]
            )
            copy.start()
            copies.append(copy)
    for copy in copies:
        copy.wait()


def expand(pieces, b_own, b_sib, place, slot, live, me):
    rows = pieces[0].shape[1] // NNZ
    share = SLOTS // NY
    grid_spec = pltpu.PrefetchScalarGridSpec(
        num_scalar_prefetch=4,
        grid=(),
        in_specs=[pl.BlockSpec(memory_space=pl.ANY)] * (len(pieces) + 2),
        out_specs=pl.BlockSpec(memory_space=pl.ANY),
        scratch_shapes=[
            pltpu.VMEM((TB, NNZ * rows, TILE), jnp.bfloat16),
            pltpu.VMEM((2, TB, TILE, TILE), jnp.bfloat16),
            pltpu.VMEM((SLOTS, rows, TILE), jnp.float32),
            pltpu.VMEM((SLOTS, rows, TILE), jnp.float32),
            pltpu.VMEM((2, NY, share, rows, TILE), jnp.bfloat16),
            pltpu.SemaphoreType.DMA((len(pieces) + 2,)),
            pltpu.SemaphoreType.DMA((2, NY)),
        ],
    )
    return pl.pallas_call(
        functools.partial(expand_kernel, rows, len(pieces)),
        out_shape=jax.ShapeDtypeStruct((2 * NY, share, rows, TILE), jnp.bfloat16),
        grid_spec=grid_spec,
        compiler_params=pltpu.CompilerParams(vmem_limit_bytes=VMEM_LIMIT),
        name="expand",
    )(place, slot, live, me, *pieces, b_own, b_sib)


def square_kernel(first, second, squared, total):
    share = SLOTS // NY
    total[...] = jnp.zeros_like(total)

    def step(i, carry):
        for source, low in ((first, 0), (second, first.shape[2])):
            rows = source.shape[2]
            for c in range(2):
                value = source[c, i].astype(jnp.float32)
                for y in range(1, NY):
                    value += source[2 * y + c, i].astype(jnp.float32)
                value = value * value
                squared[i, pl.ds(c * ROWS + low, rows)] = value
                total[pl.ds(lax.rem(i, JB_DEV), 1)] += jnp.sum(value, axis=0, keepdims=True)
        return carry

    lax.fori_loop(0, share, step, 0, unroll=2)


def square(first, second):
    share = SLOTS // NY
    return pl.pallas_call(
        square_kernel,
        out_shape=(
            jax.ShapeDtypeStruct((share, TILE, TILE), jnp.float32),
            jax.ShapeDtypeStruct((JB_DEV, TILE), jnp.float32),
        ),
        in_specs=[pl.BlockSpec(memory_space=pltpu.VMEM)] * 2,
        out_specs=[pl.BlockSpec(memory_space=pltpu.VMEM)] * 2,
        compiler_params=pltpu.CompilerParams(vmem_limit_bytes=VMEM_LIMIT),
        name="square",
    )(first, second)


def per_device(a_tiles, b_tiles, b_block, c_slot, b_live):
    x, z, core = lax.axis_index("x"), lax.axis_index("z"), lax.axis_index("c")
    kept = lax.dynamic_slice_in_dim(a_tiles, core * ROWS, ROWS, 2)
    given = lax.dynamic_slice_in_dim(a_tiles, (1 - core) * ROWS, ROWS, 2)
    pair = jnp.concatenate([kept, shift(given, "c", 1)])
    first = pair[:, :, :FIRST].reshape(2, NNZ * FIRST, TILE)
    second = pair[:, :, FIRST:].reshape(2, NNZ * (ROWS - FIRST), TILE)
    b_own = b_tiles[0]
    b_sib = shift(b_own, "c", 1)
    table = jnp.concatenate(
        [b_block[0][:, None], c_slot[0], jnp.broadcast_to(b_live, (TB, 1))], axis=1
    )
    table = jnp.concatenate([table, shift(table, "c", 1)])
    block, slot = table[:, 0], table[:, 1 : 1 + NNZ].reshape(-1)
    live = table[::TB, 1 + NNZ]
    x_at = ring_place((x - block // (2 * NZ)) % NX, NX)
    z_at = ring_place((z - (block // 2) % NZ) % NZ, NZ)
    c_at = (block + core) % 2
    me = core[None].astype(jnp.int32)
    first_pieces, second_pieces = gather_left(first, second)
    part1 = expand(first_pieces, b_own, b_sib, (z_at * NX + x_at) * 2 + c_at, slot, live, me)
    part2 = expand(second_pieces, b_own, b_sib, (x_at * NZ + z_at) * 2 + c_at, slot, live, me)
    part1 = lax.all_to_all(part1, ("y", "c"), 0, 0, tiled=True)
    part2 = lax.all_to_all(part2, ("y", "c"), 0, 0, tiled=True)
    squared, column_part = square(part1, part2)
    column_total = lax.psum(column_part, "y")
    factor = (OUT_J * TILE) / column_total
    share = SLOTS // NY
    inflated = squared.reshape(share // JB_DEV, JB_DEV, TILE, TILE) * factor[None, :, None, :]
    return inflated.reshape(share, 1, TILE, TILE).astype(jnp.bfloat16)


def solution(mesh):
    fine = Mesh(mesh.devices.reshape(NY, NX, NZ, 2), ("y", "x", "z", "c"))
    col = ("x", "z", "c")
    in_specs = (
        P(("y",) + col, None, None, None),
        P("y", col, None, None),
        P("y", col),
        P("y", col, None),
        P("y", col),
    )
    out_specs = P("y", col, None, None)
    return jax.shard_map(
        per_device, mesh=fine, in_specs=in_specs, out_specs=out_specs, check_vma=False
    )
```

```python
import functools

import jax
import jax.numpy as jnp
from jax import lax
from jax.experimental import pallas as pl
from jax.experimental.pallas import tpu as pltpu
from jax.sharding import Mesh
from jax.sharding import PartitionSpec as P

JB_DEV = 8
OUT_J = 16
TILE = 128
NNZ = 8
TB = 64
SLOTS = 128
NX, NY, NZ = 4, 4, 8
SIZES = {"y": NY, "x": NX, "z": NZ, "c": 2}
PEERS = 2 * NY
ROWS = TILE // PEERS
SHARE = SLOTS // NY
BODY = SHARE * ROWS
TABLE = 16
UNROLL = 8
MIB = 1024 * 1024
EXTRA = 13
PIECE = pl.BlockSpec(memory_space=pl.ANY)


def shift(value, axis, step):
    n = SIZES[axis]
    return lax.ppermute(value, axis, [(i, (i + step) % n) for i in range(n)])


def ring_place(distance, n):
    return jnp.maximum(jnp.minimum(2 * distance - 1, 2 * (n - distance)), 0)


def after(value, *others):
    return lax.optimization_barrier((value, *others))[0]


def rise_and_fall(value):
    pairs = []
    for y in range(NY):
        pairs.append((2 * y, 2 * ((y + 1) % NY)))
        pairs.append((2 * y + 1, 2 * ((y - 1) % NY) + 1))
    return lax.ppermute(value, ("y", "c"), pairs)


def cross(value, step0, step1):
    pairs = []
    for x in range(NX):
        for z in range(NZ):
            for core, step in ((0, step0), (1, step1)):
                if step is not None:
                    target = ((x + step[0]) % NX * NZ + (z + step[1]) % NZ) * 2 + core
                    pairs.append(((x * NZ + z) * 2 + core, target))
    return lax.ppermute(value, ("x", "z", "c"), pairs)


def gather(piece, block, core):
    on_x = core == 0
    p1, n1 = cross(piece, (1, 0), (0, 1)), cross(piece, (-1, 0), (0, -1))
    ring1 = rise_and_fall(block)
    swap0 = shift(block, "c", 1)
    p2 = cross(jnp.where(on_x, piece, p1), (2, 0), (0, 1))
    n2 = cross(after(n1, swap0), None, (0, -1))
    base = jnp.concatenate([piece, p1, n1, p2])
    q1, m1 = cross(base, (0, 1), (1, 0)), cross(base, (0, -1), (-1, 0))
    p3, n3 = cross(p2, None, (0, 1)), cross(n2, None, (0, -1))
    ring2 = rise_and_fall(after(ring1, p3))
    p4 = cross(p3, None, (0, 1))
    rest = jnp.concatenate([n2, p3, n3, p4])
    q2 = cross(jnp.where(on_x, q1, rest), (0, 1), (1, 0))
    m2 = cross(jnp.where(on_x, m1, rest), (0, -1), (-1, 0))
    swap1 = shift(after(ring1, q1, m1), "c", 1)
    q3 = cross(jnp.where(on_x, q2, q1), (0, 1), (1, 0))
    m3 = cross(after(m2, swap1), (0, -1), (-1, 0))
    half = q3.shape[0] // 2
    q4 = cross(q3[:half], (0, 1), None)
    m4 = cross(m3[half:], (0, -1), None)
    ring3 = rise_and_fall(after(ring2, q2, m2))
    swap2 = shift(after(ring2, q3, m3), "c", 1)
    pieces = [base, q1, m1, q2, m2, q3, m3, q4, m4, rest]
    return pieces, [block, swap0, ring1, swap1, ring2, swap2], ring3


def accumulate_kernel(hops, first, last, place, slot, live, me, *refs):
    n_blocks, n_pieces, group = 2 * len(hops), 10, NX * PEERS
    pieces, refs = refs[:n_pieces], refs[n_pieces:]
    blocks, refs = refs[:n_blocks], refs[n_blocks:]
    if not first:
        before, refs = refs[:2], refs[2:]
    if last:
        out, refs = refs[0], refs[1:]
        left, right, acc0, acc1, sems, right_sems, acc_sems, packed, out_sems = refs
    else:
        acc_out, refs = refs[:2], refs[2:]
        left, right, acc0, acc1, sems, right_sems, acc_sems = refs
    row, core = me[0], me[1]
    copies = [
        pltpu.make_async_copy(pieces[n], left.at[pl.ds(n * group, group)], sems.at[n])
        for n in range(7)
    ]
    tail = (NY + 3) * group
    half0 = pltpu.make_async_copy(pieces[7], left.at[pl.ds(tail, group // 2)], sems.at[7])
    half1 = pltpu.make_async_copy(
        pieces[8], left.at[pl.ds(tail + group // 2, group // 2)], sems.at[8]
    )
    rest = pltpu.make_async_copy(pieces[9], left.at[pl.ds(tail, group)], sems.at[9])
    right_copies = [
        pltpu.make_async_copy(block, right.at[n], right_sems.at[n])
        for n, block in enumerate(blocks)
    ]
    for copy in copies:
        copy.start()

    @pl.when(core == 0)
    def _():
        half0.start()
        half1.start()

    @pl.when(core == 1)
    def _():
        rest.start()

    for copy in right_copies:
        copy.start()
    if first:

        def clear(i, carry):
            acc0[i] = jnp.zeros((ROWS, TILE), jnp.float32)
            acc1[i] = jnp.zeros((ROWS, TILE), jnp.float32)
            return carry

        lax.fori_loop(0, SLOTS, clear, 0, unroll=8)
    else:
        acc_copies = [
            pltpu.make_async_copy(source, acc, acc_sems.at[n])
            for n, (source, acc) in enumerate(zip(before, (acc0, acc1)))
        ]
        for copy in acc_copies:
            copy.start()
        for copy in acc_copies:
            copy.wait()
    for copy in copies:
        copy.wait()

    @pl.when(core == 0)
    def _():
        half0.wait()
        half1.wait()

    @pl.when(core == 1)
    def _():
        rest.wait()

    zero = jnp.zeros((TILE, TILE), jnp.bfloat16)

    def multiply(n, source, t):
        right_block = jnp.where(t < live[source], right[n, t], zero)
        return jnp.dot(
            left[place[source * TB + t]], right_block, preferred_element_type=jnp.float32
        )

    for n, hop in enumerate(hops):
        down, up = lax.rem(row + NY - hop, NY), lax.rem(row + hop, NY)
        own = 2 * jnp.where(core == 0, down, up) + core
        sib = 2 * jnp.where(core == 0, up, down) + 1 - core
        right_copies[2 * n].wait()
        right_copies[2 * n + 1].wait()

        def step(s, carry, n=n, own=own, sib=sib):
            slots = [UNROLL * s + u for u in range(UNROLL)]
            products = [(multiply(2 * n, own, t), multiply(2 * n + 1, sib, t)) for t in slots]
            for t, (mine, other) in zip(slots, products):
                for m in range(NNZ):
                    part = slice(m * ROWS, (m + 1) * ROWS)
                    acc0[slot[(own * TB + t) * NNZ + m]] += mine[part]
                    acc1[slot[(sib * TB + t) * NNZ + m]] += other[part]
            return carry

        steps = (jnp.maximum(live[own], live[sib]) + UNROLL - 1) // UNROLL
        lax.fori_loop(0, steps, step, 0)

    if not last:
        acc_copies = [
            pltpu.make_async_copy(acc, target, acc_sems.at[n])
            for n, (acc, target) in enumerate(zip((acc0, acc1), acc_out))
        ]
        for copy in acc_copies:
            copy.start()
        for copy in acc_copies:
            copy.wait()
        return
    copies = []
    for q, acc in ((0, acc0), (1, acc1)):
        totals = [jnp.zeros((1, TILE), jnp.float32)] * JB_DEV
        for y in range(NY):

            def narrow(k, totals, q=q, y=y, acc=acc):
                totals = list(totals)
                for j in range(JB_DEV):
                    value = acc[y * SHARE + k * JB_DEV + j]
                    value = value * value
                    at = pl.multiple_of((k * JB_DEV + j) * ROWS, ROWS)
                    packed[q, y, pl.ds(at, ROWS)] = value.astype(jnp.bfloat16)
                    totals[j] = totals[j] + jnp.sum(value, axis=0, keepdims=True)
                return tuple(totals)

            totals = lax.fori_loop(0, SHARE // JB_DEV, narrow, tuple(totals))
        total = jnp.concatenate(totals, axis=0)
        high = total.astype(jnp.bfloat16)
        low = (total - high.astype(jnp.float32)).astype(jnp.bfloat16)
        for y in range(NY):
            packed[q, y, pl.ds(BODY, JB_DEV)] = high
            packed[q, y, pl.ds(BODY + JB_DEV, JB_DEV)] = low
            copy = pltpu.make_async_copy(
                packed.at[q, y], out.at[2 * y + jnp.bitwise_xor(core, q)], out_sems.at[q, y]
            )
            copy.start()
            copies.append(copy)
    for copy in copies:
        copy.wait()


def accumulate(hops, pieces, blocks, before, last, tables):
    n_inputs = len(pieces) + len(blocks) + len(before)
    anywhere = pl.BlockSpec(memory_space=pl.ANY)
    acc = jax.ShapeDtypeStruct((SLOTS, ROWS, TILE), jnp.float32)
    scratch = [
        pltpu.VMEM((NX * NZ * PEERS, NNZ * ROWS, TILE), jnp.bfloat16),
        pltpu.VMEM((len(blocks), TB, TILE, TILE), jnp.bfloat16),
        pltpu.VMEM((SLOTS, ROWS, TILE), jnp.float32),
        pltpu.VMEM((SLOTS, ROWS, TILE), jnp.float32),
        pltpu.SemaphoreType.DMA((len(pieces),)),
        pltpu.SemaphoreType.DMA((len(blocks),)),
        pltpu.SemaphoreType.DMA((2,)),
    ]
    if last:
        scratch += [
            pltpu.VMEM((2, NY, BODY + 2 * JB_DEV, TILE), jnp.bfloat16),
            pltpu.SemaphoreType.DMA((2, NY)),
        ]
    grid_spec = pltpu.PrefetchScalarGridSpec(
        num_scalar_prefetch=4,
        grid=(),
        in_specs=[PIECE] * len(pieces) + [anywhere] * (n_inputs - len(pieces)),
        out_specs=anywhere if last else (anywhere, anywhere),
        scratch_shapes=scratch,
    )
    return pl.pallas_call(
        functools.partial(accumulate_kernel, hops, not before, last),
        out_shape=jax.ShapeDtypeStruct((PEERS, BODY + 2 * JB_DEV, TILE), jnp.bfloat16)
        if last
        else (acc, acc),
        grid_spec=grid_spec,
        compiler_params=pltpu.CompilerParams(vmem_limit_bytes=(EXTRA + 2 * len(blocks)) * MIB),
        name="accumulate",
    )(*tables, *pieces, *blocks, *before)


def inflate_kernel(source, out):
    total = jnp.zeros((JB_DEV, TILE), jnp.float32)
    for peer in range(PEERS):
        total += source[peer, BODY : BODY + JB_DEV].astype(jnp.float32)
        total += source[peer, BODY + JB_DEV : BODY + 2 * JB_DEV].astype(jnp.float32)
    factor = (OUT_J * TILE) / total
    for j in range(JB_DEV):
        scale = factor[j : j + 1]
        for k in range(SHARE // JB_DEV):
            i = k * JB_DEV + j
            for peer in range(PEERS):
                value = source[peer, i * ROWS : (i + 1) * ROWS].astype(jnp.float32)
                out[i, 0, peer * ROWS : (peer + 1) * ROWS] = (value * scale).astype(jnp.bfloat16)


def inflate(source):
    return pl.pallas_call(
        inflate_kernel,
        out_shape=jax.ShapeDtypeStruct((SHARE, 1, TILE, TILE), jnp.bfloat16),
        in_specs=[pl.BlockSpec(memory_space=pltpu.VMEM)],
        out_specs=pl.BlockSpec(memory_space=pltpu.VMEM),
        compiler_params=pltpu.CompilerParams(vmem_limit_bytes=12 * MIB),
        name="inflate",
    )(source)


def per_device(a_tiles, b_tiles, b_block, c_slot, b_live):
    y, x, z, core = (lax.axis_index(axis) for axis in ("y", "x", "z", "c"))
    rows = a_tiles.reshape(NNZ, PEERS, ROWS, TILE).transpose(1, 0, 2, 3)
    rows = rows.reshape(PEERS, NNZ * ROWS, TILE)
    table = jnp.concatenate(
        [b_block[0], c_slot[0].reshape(-1), jnp.broadcast_to(b_live[0], (TB,))]
    ).astype(jnp.bfloat16)
    table = jnp.pad(table, (0, TABLE * TILE - table.shape[0])).reshape(1, TABLE, TILE)
    dealt = jnp.concatenate([rows, jnp.broadcast_to(table, (PEERS, TABLE, TILE))], axis=1)
    dealt = lax.all_to_all(dealt, ("y", "c"), 0, 0, tiled=True)
    piece = dealt[:, : NNZ * ROWS]
    table = dealt[:, NNZ * ROWS :].reshape(PEERS, TABLE * TILE).astype(jnp.int32)
    block, live = table[:, :TB], table[:, TB * (1 + NNZ)]
    slot = table[:, TB : TB * (1 + NNZ)].reshape(-1)
    x_at = ring_place((x - block // (2 * NZ)) % NX, NX)
    z_at = ring_place((z - (block // 2) % NZ) % NZ, NZ)
    source = jnp.arange(PEERS, dtype=jnp.int32)[:, None] // 2 * 2 + block % 2
    low = jnp.where(x_at == 3, 5, x_at)
    high = jnp.where(x_at == 0, 7, jnp.where(x_at == 3, 6, x_at + 2))
    group = jnp.where(core == 0, z_at, jnp.where(z_at < NX, low, high))
    within = jnp.where(core == 0, x_at, z_at % NX)
    place = ((group * NX + within) * PEERS + source).reshape(-1)
    me = jnp.stack([y, core]).astype(jnp.int32)
    pieces, blocks, last = gather(piece, after(b_tiles[0], dealt), core)
    tables = (place, slot, live, me)
    early, late = tuple(range(NY - 1)), (NY - 1,)
    before = accumulate(early, pieces, blocks, (), False, tables)
    blocks = [last, shift(after(last, *before), "c", 1)]
    packed = accumulate(late, pieces, blocks, before, True, tables)
    return inflate(lax.all_to_all(packed, ("y", "c"), 0, 0, tiled=True))


def solution(mesh):
    fine = Mesh(mesh.devices.reshape(NY, NX, NZ, 2), ("y", "x", "z", "c"))
    col = ("x", "z", "c")
    in_specs = (
        P(("y",) + col, None, None, None),
        P("y", col, None, None),
        P("y", col),
        P("y", col, None),
        P("y", col),
    )
    out_specs = P("y", col, None, None)
    return jax.shard_map(
        per_device, mesh=fine, in_specs=in_specs, out_specs=out_specs, check_vma=False
    )
```

```python
import functools

import jax
import jax.numpy as jnp
from jax import lax
from jax.experimental import pallas as pl
from jax.experimental.pallas import tpu as pltpu
from jax.sharding import Mesh
from jax.sharding import PartitionSpec as P

JB_DEV = 8
OUT_J = 16
TILE = 128
NNZ = 8
TB = 64
SLOTS = 128
NX, NY, NZ = 4, 4, 8
SIZES = {"y": NY, "x": NX, "z": NZ, "c": 2}
PEERS = 2 * NY
ROWS = TILE // PEERS
SHARE = SLOTS // NY
BODY = SHARE * ROWS
TABLE = 16
UNROLL = 8
MIB = 1024 * 1024
KEPT = pltpu.HBM


def shift(value, axis, step):
    n = SIZES[axis]
    return lax.ppermute(value, axis, [(i, (i + step) % n) for i in range(n)])


def ring_place(distance, n):
    return jnp.maximum(jnp.minimum(2 * distance - 1, 2 * (n - distance)), 0)


def after(value, *others):
    return lax.optimization_barrier((value, *others))[0]


def rise_and_fall(value):
    pairs = []
    for y in range(NY):
        pairs.append((2 * y, 2 * ((y + 1) % NY)))
        pairs.append((2 * y + 1, 2 * ((y - 1) % NY) + 1))
    return lax.ppermute(value, ("y", "c"), pairs)


def cross(value, step0, step1):
    pairs = []
    for x in range(NX):
        for z in range(NZ):
            for core, step in ((0, step0), (1, step1)):
                if step is not None:
                    target = ((x + step[0]) % NX * NZ + (z + step[1]) % NZ) * 2 + core
                    pairs.append(((x * NZ + z) * 2 + core, target))
    return lax.ppermute(value, ("x", "z", "c"), pairs)


def gather(piece, block, core):
    on_x = core == 0
    p1, n1 = cross(piece, (1, 0), (0, 1)), cross(piece, (-1, 0), (0, -1))
    ring1 = rise_and_fall(block)
    swap0 = shift(block, "c", 1)
    p2 = cross(jnp.where(on_x, piece, p1), (2, 0), (0, 1))
    n2 = cross(after(n1, swap0), None, (0, -1))
    base = jnp.concatenate([piece, p1, n1, p2])
    q1, m1 = cross(base, (0, 1), (1, 0)), cross(base, (0, -1), (-1, 0))
    p3, n3 = cross(p2, None, (0, 1)), cross(n2, None, (0, -1))
    ring2 = rise_and_fall(after(ring1, p3))
    p4 = cross(p3, None, (0, 1))
    rest = jnp.concatenate([n2, p3, n3, p4])
    q2 = cross(jnp.where(on_x, q1, rest), (0, 1), (1, 0))
    m2 = cross(jnp.where(on_x, m1, rest), (0, -1), (-1, 0))
    swap1 = shift(after(ring1, q1, m1), "c", 1)
    q3 = cross(jnp.where(on_x, q2, q1), (0, 1), (1, 0))
    m3 = cross(after(m2, swap1), (0, -1), (-1, 0))
    half = q2.shape[0] // 2
    q4 = cross(q2[:half], (0, 2), None)
    m4 = cross(m2[half:], (0, -2), None)
    ring3 = rise_and_fall(after(ring2, m2))
    swap2 = shift(after(ring2, q3, m3), "c", 1)
    swap3 = shift(after(ring3, q4, m4), "c", 1)
    blocks = [block, swap0, ring1, swap1, ring2, swap2, ring3, swap3]
    return [base, q1, m1, q2, m2, q3, m3, q4, m4, rest], blocks


def accumulate_kernel(place, slot, live, me, *refs):
    group = NX * PEERS
    pieces, blocks, out = refs[:10], refs[10 : 10 + PEERS], refs[10 + PEERS]
    left, right, acc0, acc1, packed, sems, right_sems, out_sems = refs[11 + PEERS :]
    row, core = me[0], me[1]
    targets = [left.at[pl.ds(n * group, group)] for n in range(7)]
    targets += [left.at[pl.ds(7 * group + n * group // 2, group // 2)] for n in range(2)]
    targets += [left.at[pl.ds(7 * group, group)]]
    copies = [
        pltpu.make_async_copy(piece, target, sems.at[n])
        for n, (piece, target) in enumerate(zip(pieces, targets))
    ]
    right_copies = [
        pltpu.make_async_copy(block, right.at[n], right_sems.at[n])
        for n, block in enumerate(blocks)
    ]
    for copy in right_copies[:2] + copies[:7]:
        copy.start()
    for which, copy in ((0, copies[7]), (0, copies[8]), (1, copies[9])):
        pl.when(core == which)(copy.start)
    for copy in right_copies[2:]:
        copy.start()

    def clear(i, carry):
        acc0[i] = jnp.zeros((ROWS, TILE), jnp.float32)
        acc1[i] = jnp.zeros((ROWS, TILE), jnp.float32)
        return carry

    lax.fori_loop(0, SLOTS, clear, 0, unroll=8)
    for copy in copies[:7]:
        copy.wait()
    for which, copy in ((0, copies[7]), (0, copies[8]), (1, copies[9])):
        pl.when(core == which)(copy.wait)
    def multiply(n, source, t):
        return jnp.dot(
            left[place[source * TB + t]], right[n, t], preferred_element_type=jnp.float32
        )

    def steps(panels, first, last):
        def step(s, carry):
            slots = [UNROLL * s + u for u in range(UNROLL)]
            products = [[multiply(n, source, t) for n, source, _ in panels] for t in slots]
            for t, values in zip(slots, products):
                for m in range(NNZ):
                    for (_, source, acc), value in zip(panels, values):
                        at = slot[(source * TB + t) * NNZ + m]
                        acc[at] += value[m * ROWS : (m + 1) * ROWS]
            return carry

        lax.fori_loop(first, last, step, 0)

    for hop in range(NY):
        down, up = lax.rem(row + NY - hop, NY), lax.rem(row + hop, NY)
        own = 2 * jnp.where(core == 0, down, up) + core
        sib = 2 * jnp.where(core == 0, up, down) + 1 - core
        right_copies[2 * hop].wait()
        right_copies[2 * hop + 1].wait()
        own_panel, sib_panel = (2 * hop, own, acc0), (2 * hop + 1, sib, acc1)
        own_steps = (live[own] + UNROLL - 1) // UNROLL
        sib_steps = (live[sib] + UNROLL - 1) // UNROLL
        shared = jnp.minimum(own_steps, sib_steps)
        steps((own_panel, sib_panel), 0, shared)
        steps((own_panel,), shared, own_steps)
        steps((sib_panel,), shared, sib_steps)

    copies = []
    for q, acc in ((0, acc0), (1, acc1)):
        totals = [jnp.zeros((8, TILE), jnp.float32)] * JB_DEV
        for y in range(NY):

            def narrow(k, totals, q=q, y=y, acc=acc):
                totals = list(totals)
                for j in range(JB_DEV):
                    value = acc[y * SHARE + k * JB_DEV + j]
                    value = value * value
                    at = pl.multiple_of((k * JB_DEV + j) * ROWS, ROWS)
                    packed[q, y, pl.ds(at, ROWS)] = value.astype(jnp.bfloat16)
                    totals[j] = totals[j] + value[:8] + value[8:]
                return tuple(totals)

            totals = lax.fori_loop(0, SHARE // JB_DEV, narrow, tuple(totals))
        total = jnp.concatenate(
            [jnp.sum(value, axis=0, keepdims=True) for value in totals], axis=0
        )
        high = total.astype(jnp.bfloat16)
        low = (total - high.astype(jnp.float32)).astype(jnp.bfloat16)
        for y in range(NY):
            packed[q, y, pl.ds(BODY, JB_DEV)] = high
            packed[q, y, pl.ds(BODY + JB_DEV, JB_DEV)] = low
            copy = pltpu.make_async_copy(
                packed.at[q, y], out.at[2 * y + jnp.bitwise_xor(core, q)], out_sems.at[q, y]
            )
            copy.start()
            copies.append(copy)
    for copy in copies:
        copy.wait()


def accumulate(pieces, blocks, tables):
    kept = pl.BlockSpec(memory_space=KEPT)
    grid_spec = pltpu.PrefetchScalarGridSpec(
        num_scalar_prefetch=4,
        grid=(),
        in_specs=[kept] * (len(pieces) + len(blocks)),
        out_specs=pl.BlockSpec(memory_space=pl.ANY),
        scratch_shapes=[
            pltpu.VMEM((NX * NZ * PEERS, NNZ * ROWS, TILE), jnp.bfloat16),
            pltpu.VMEM((PEERS, TB, TILE, TILE), jnp.bfloat16),
            pltpu.VMEM((SLOTS + 1, ROWS, TILE), jnp.float32),
            pltpu.VMEM((SLOTS + 1, ROWS, TILE), jnp.float32),
            pltpu.VMEM((2, NY, BODY + 2 * JB_DEV, TILE), jnp.bfloat16),
            pltpu.SemaphoreType.DMA((len(pieces),)),
            pltpu.SemaphoreType.DMA((PEERS,)),
            pltpu.SemaphoreType.DMA((2, NY)),
        ],
    )
    return pl.pallas_call(
        accumulate_kernel,
        out_shape=jax.ShapeDtypeStruct((PEERS, BODY + 2 * JB_DEV, TILE), jnp.bfloat16),
        grid_spec=grid_spec,
        compiler_params=pltpu.CompilerParams(vmem_limit_bytes=60 * MIB),
        name="accumulate",
    )(*tables, *pieces, *blocks)


def inflate_kernel(source, out):
    total = jnp.zeros((JB_DEV, TILE), jnp.float32)
    for peer in range(PEERS):
        total += source[peer, BODY : BODY + JB_DEV].astype(jnp.float32)
        total += source[peer, BODY + JB_DEV : BODY + 2 * JB_DEV].astype(jnp.float32)
    factor = (OUT_J * TILE) / total
    for j in range(JB_DEV):
        scale = factor[j : j + 1]
        for k in range(SHARE // JB_DEV):
            i = k * JB_DEV + j
            for peer in range(PEERS):
                value = source[peer, i * ROWS : (i + 1) * ROWS].astype(jnp.float32)
                out[i, 0, peer * ROWS : (peer + 1) * ROWS] = (value * scale).astype(jnp.bfloat16)


def inflate(source):
    return pl.pallas_call(
        inflate_kernel,
        out_shape=jax.ShapeDtypeStruct((SHARE, 1, TILE, TILE), jnp.bfloat16),
        in_specs=[pl.BlockSpec(memory_space=pltpu.VMEM)],
        out_specs=pl.BlockSpec(memory_space=pltpu.VMEM),
        compiler_params=pltpu.CompilerParams(vmem_limit_bytes=12 * MIB),
        name="inflate",
    )(source)


def per_device(a_tiles, b_tiles, b_block, c_slot, b_live):
    y, x, z, core = (lax.axis_index(axis) for axis in ("y", "x", "z", "c"))
    rows = a_tiles.reshape(NNZ, PEERS, ROWS, TILE).transpose(1, 0, 2, 3)
    rows = rows.reshape(PEERS, NNZ * ROWS, TILE)
    table = jnp.concatenate(
        [b_block[0], c_slot[0].reshape(-1), jnp.broadcast_to(b_live[0], (TB,))]
    ).astype(jnp.bfloat16)
    table = jnp.pad(table, (0, TABLE * TILE - table.shape[0])).reshape(1, TABLE, TILE)
    dealt = jnp.concatenate([rows, jnp.broadcast_to(table, (PEERS, TABLE, TILE))], axis=1)
    dealt = lax.all_to_all(dealt, ("y", "c"), 0, 0, tiled=True)
    piece = dealt[:, : NNZ * ROWS]
    table = dealt[:, NNZ * ROWS :].reshape(PEERS, TABLE * TILE).astype(jnp.int32)
    block, live = table[:, :TB], table[:, TB * (1 + NNZ)]
    slot = table[:, TB : TB * (1 + NNZ)].reshape(PEERS, TB, NNZ)
    dead = jnp.arange(TB, dtype=jnp.int32)[None, :, None] >= live[:, None, None]
    slot = jnp.where(dead, SLOTS, slot).reshape(-1)
    x_at = ring_place((x - block // (2 * NZ)) % NX, NX)
    z_at = ring_place((z - (block // 2) % NZ) % NZ, NZ)
    source = jnp.arange(PEERS, dtype=jnp.int32)[:, None] // 2 * 2 + block % 2
    low = jnp.where(x_at == 3, 5, x_at)
    high = jnp.where(x_at == 0, 7, jnp.where(x_at == 3, 6, x_at + 2))
    group = jnp.where(core == 0, z_at, jnp.where(z_at < NX, low, high))
    within = jnp.where(core == 0, x_at, z_at % NX)
    place = ((group * NX + within) * PEERS + source).reshape(-1)
    me = jnp.stack([y, core]).astype(jnp.int32)
    pieces, blocks = gather(piece, after(b_tiles[0], dealt), core)
    packed = accumulate(pieces, blocks, (place, slot, live, me))
    return inflate(lax.all_to_all(packed, ("y", "c"), 0, 0, tiled=True))


def solution(mesh):
    fine = Mesh(mesh.devices.reshape(NY, NX, NZ, 2), ("y", "x", "z", "c"))
    col = ("x", "z", "c")
    in_specs = (
        P(("y",) + col, None, None, None),
        P("y", col, None, None),
        P("y", col),
        P("y", col, None),
        P("y", col),
    )
    out_specs = P("y", col, None, None)
    return jax.shard_map(
        per_device, mesh=fine, in_specs=in_specs, out_specs=out_specs, check_vma=False
    )
```

```python
import functools

import jax
import jax.numpy as jnp
from jax import lax
from jax.experimental import pallas as pl
from jax.experimental.pallas import tpu as pltpu
from jax.sharding import Mesh
from jax.sharding import PartitionSpec as P

JB_DEV = 8
OUT_J = 16
TILE = 128
NNZ = 8
TB = 64
SLOTS = 128
NX, NY, NZ = 4, 4, 8
SIZES = {"y": NY, "x": NX, "z": NZ, "c": 2}
PEERS = 2 * NY
ROWS = TILE // PEERS
SHARE = SLOTS // NY
BODY = SHARE * ROWS
TABLE = 16
UNROLL = 8
MIB = 1024 * 1024
KEPT = pltpu.HBM


def shift(value, axis, step):
    n = SIZES[axis]
    return lax.ppermute(value, axis, [(i, (i + step) % n) for i in range(n)])


def ring_place(distance, n):
    return jnp.maximum(jnp.minimum(2 * distance - 1, 2 * (n - distance)), 0)


def after(value, *others):
    return lax.optimization_barrier((value, *others))[0]


def rise_and_fall(value):
    pairs = []
    for y in range(NY):
        pairs.append((2 * y, 2 * ((y + 1) % NY)))
        pairs.append((2 * y + 1, 2 * ((y - 1) % NY) + 1))
    return lax.ppermute(value, ("y", "c"), pairs)


def cross(value, step0, step1):
    pairs = []
    for x in range(NX):
        for z in range(NZ):
            for core, step in ((0, step0), (1, step1)):
                if step is not None:
                    target = ((x + step[0]) % NX * NZ + (z + step[1]) % NZ) * 2 + core
                    pairs.append(((x * NZ + z) * 2 + core, target))
    return lax.ppermute(value, ("x", "z", "c"), pairs)


def gather(piece, block, core):
    on_x = core == 0
    p1, n1 = cross(piece, (1, 0), (0, 1)), cross(piece, (-1, 0), (0, -1))
    ring1 = rise_and_fall(block)
    swap0 = shift(block, "c", 1)
    p2 = cross(jnp.where(on_x, piece, p1), (2, 0), (0, 1))
    n2 = cross(after(n1, swap0), None, (0, -1))
    base = jnp.concatenate([piece, p1, n1, p2])
    q1, m1 = cross(base, (0, 1), (1, 0)), cross(base, (0, -1), (-1, 0))
    p3, n3 = cross(p2, None, (0, 1)), cross(n2, None, (0, -1))
    ring2 = rise_and_fall(after(ring1, p3))
    p4 = cross(p3, None, (0, 1))
    rest = jnp.concatenate([n2, p3, n3, p4])
    q2 = cross(jnp.where(on_x, q1, rest), (0, 1), (1, 0))
    m2 = cross(jnp.where(on_x, m1, rest), (0, -1), (-1, 0))
    swap1 = shift(after(ring1, q1, m1), "c", 1)
    q3 = cross(jnp.where(on_x, q2, q1), (0, 1), (1, 0))
    m3 = cross(after(m2, swap1), (0, -1), (-1, 0))
    half = q2.shape[0] // 2
    q4 = cross(q2[:half], (0, 2), None)
    m4 = cross(m2[half:], (0, -2), None)
    ring3 = rise_and_fall(after(ring2, m2))
    swap2 = shift(after(ring2, q3, m3), "c", 1)
    swap3 = shift(after(ring3, q4, m4), "c", 1)
    blocks = [block, swap0, ring1, swap1, ring2, swap2, ring3, swap3]
    return [base, q1, m1, q2, m2, q3, m3, q4, m4, rest], blocks


def accumulate_kernel(place, slot, live, me, *refs):
    group = NX * PEERS
    pieces, blocks, out = refs[:10], refs[10 : 10 + PEERS], refs[10 + PEERS]
    left, right, acc0, acc1, odd0, odd1, packed, sems, right_sems, out_sems = refs[11 + PEERS :]
    row, core = me[0], me[1]
    targets = [left.at[pl.ds(n * group, group)] for n in range(7)]
    targets += [left.at[pl.ds(7 * group + n * group // 2, group // 2)] for n in range(2)]
    targets += [left.at[pl.ds(7 * group, group)]]
    copies = [
        pltpu.make_async_copy(piece, target, sems.at[n])
        for n, (piece, target) in enumerate(zip(pieces, targets))
    ]
    right_copies = [
        pltpu.make_async_copy(block, right.at[n], right_sems.at[n])
        for n, block in enumerate(blocks)
    ]
    for copy in right_copies[:2] + copies[:7]:
        copy.start()
    for which, copy in ((0, copies[7]), (0, copies[8]), (1, copies[9])):
        pl.when(core == which)(copy.start)

    def clear(i, carry):
        acc0[i] = jnp.zeros((ROWS, TILE), jnp.float32)
        acc1[i] = jnp.zeros((ROWS, TILE), jnp.float32)
        odd0[i] = jnp.zeros((ROWS, TILE), jnp.float32)
        odd1[i] = jnp.zeros((ROWS, TILE), jnp.float32)
        return carry

    lax.fori_loop(0, SLOTS, clear, 0, unroll=8)
    for copy in copies[:7]:
        copy.wait()
    for which, copy in ((0, copies[7]), (0, copies[8]), (1, copies[9])):
        pl.when(core == which)(copy.wait)
    def multiply(n, source, t):
        return jnp.dot(
            left[place[source * TB + t]], right[n, t], preferred_element_type=jnp.float32
        )

    def steps(panels, first, last):
        def step(s, carry):
            slots = [UNROLL * s + u for u in range(UNROLL)]
            products = [[multiply(n, source, t) for n, source, _ in panels] for t in slots]
            for u in range(0, UNROLL, 2):
                for m in range(NNZ):
                    for parity in range(2):
                        for (_, source, accs), value in zip(panels, products[u + parity]):
                            at = slot[(source * NNZ + m) * TB + slots[u + parity]]
                            accs[parity][at] += value[m * ROWS : (m + 1) * ROWS]
            return carry

        lax.fori_loop(first, last, step, 0)

    for hop in range(NY):
        down, up = lax.rem(row + NY - hop, NY), lax.rem(row + hop, NY)
        own = 2 * jnp.where(core == 0, down, up) + core
        sib = 2 * jnp.where(core == 0, up, down) + 1 - core
        right_copies[2 * hop].wait()
        right_copies[2 * hop + 1].wait()
        if hop + 1 < NY:
            right_copies[2 * hop + 2].start()
            right_copies[2 * hop + 3].start()
        own_panel, sib_panel = (2 * hop, own, (acc0, odd0)), (2 * hop + 1, sib, (acc1, odd1))
        own_steps = (live[own] + UNROLL - 1) // UNROLL
        sib_steps = (live[sib] + UNROLL - 1) // UNROLL
        shared = jnp.minimum(own_steps, sib_steps)
        steps((own_panel, sib_panel), 0, shared)
        steps((own_panel,), shared, own_steps)
        steps((sib_panel,), shared, sib_steps)

    copies = []
    for q, acc, odd in ((0, acc0, odd0), (1, acc1, odd1)):
        totals = [jnp.zeros((8, TILE), jnp.float32)] * JB_DEV
        for y in range(NY):

            def narrow(k, totals, q=q, y=y, acc=acc, odd=odd):
                totals = list(totals)
                for j in range(JB_DEV):
                    value = acc[y * SHARE + k * JB_DEV + j] + odd[y * SHARE + k * JB_DEV + j]
                    value = value * value
                    at = pl.multiple_of((k * JB_DEV + j) * ROWS, ROWS)
                    packed[q, y, pl.ds(at, ROWS)] = value.astype(jnp.bfloat16)
                    totals[j] = totals[j] + value[:8] + value[8:]
                return tuple(totals)

            totals = lax.fori_loop(0, SHARE // JB_DEV, narrow, tuple(totals))
        total = jnp.concatenate(
            [jnp.sum(value, axis=0, keepdims=True) for value in totals], axis=0
        )
        high = total.astype(jnp.bfloat16)
        low = (total - high.astype(jnp.float32)).astype(jnp.bfloat16)
        for y in range(NY):
            packed[q, y, pl.ds(BODY, JB_DEV)] = high
            packed[q, y, pl.ds(BODY + JB_DEV, JB_DEV)] = low
            copy = pltpu.make_async_copy(
                packed.at[q, y], out.at[2 * y + jnp.bitwise_xor(core, q)], out_sems.at[q, y]
            )
            copy.start()
            copies.append(copy)
    for copy in copies:
        copy.wait()


def accumulate(pieces, blocks, tables):
    kept = pl.BlockSpec(memory_space=KEPT)
    grid_spec = pltpu.PrefetchScalarGridSpec(
        num_scalar_prefetch=4,
        grid=(),
        in_specs=[kept] * (len(pieces) + len(blocks)),
        out_specs=pl.BlockSpec(memory_space=pl.ANY),
        scratch_shapes=[
            pltpu.VMEM((NX * NZ * PEERS, NNZ * ROWS, TILE), jnp.bfloat16),
            pltpu.VMEM((PEERS, TB, TILE, TILE), jnp.bfloat16),
            *[pltpu.VMEM((SLOTS + 1, ROWS, TILE), jnp.float32)] * 4,
            pltpu.VMEM((2, NY, BODY + 2 * JB_DEV, TILE), jnp.bfloat16),
            pltpu.SemaphoreType.DMA((len(pieces),)),
            pltpu.SemaphoreType.DMA((PEERS,)),
            pltpu.SemaphoreType.DMA((2, NY)),
        ],
    )
    return pl.pallas_call(
        accumulate_kernel,
        out_shape=jax.ShapeDtypeStruct((PEERS, BODY + 2 * JB_DEV, TILE), jnp.bfloat16),
        grid_spec=grid_spec,
        compiler_params=pltpu.CompilerParams(vmem_limit_bytes=60 * MIB),
        name="accumulate",
    )(*tables, *pieces, *blocks)


def inflate_kernel(source, out):
    total = jnp.zeros((JB_DEV, TILE), jnp.float32)
    for peer in range(PEERS):
        total += source[peer, BODY : BODY + JB_DEV].astype(jnp.float32)
        total += source[peer, BODY + JB_DEV : BODY + 2 * JB_DEV].astype(jnp.float32)
    factor = (OUT_J * TILE) / total
    for j in range(JB_DEV):
        scale = factor[j : j + 1]
        for k in range(SHARE // JB_DEV):
            i = k * JB_DEV + j
            for peer in range(PEERS):
                value = source[peer, i * ROWS : (i + 1) * ROWS].astype(jnp.float32)
                out[i, 0, peer * ROWS : (peer + 1) * ROWS] = (value * scale).astype(jnp.bfloat16)


def inflate(source):
    return pl.pallas_call(
        inflate_kernel,
        out_shape=jax.ShapeDtypeStruct((SHARE, 1, TILE, TILE), jnp.bfloat16),
        in_specs=[pl.BlockSpec(memory_space=pltpu.VMEM)],
        out_specs=pl.BlockSpec(memory_space=pltpu.VMEM),
        compiler_params=pltpu.CompilerParams(vmem_limit_bytes=12 * MIB),
        name="inflate",
    )(source)


def per_device(a_tiles, b_tiles, b_block, c_slot, b_live):
    y, x, z, core = (lax.axis_index(axis) for axis in ("y", "x", "z", "c"))
    rows = a_tiles.reshape(NNZ, PEERS, ROWS, TILE).transpose(1, 0, 2, 3)
    rows = rows.reshape(PEERS, NNZ * ROWS, TILE)
    table = jnp.concatenate(
        [b_block[0], c_slot[0].T.reshape(-1), jnp.broadcast_to(b_live[0], (TB,))]
    ).astype(jnp.bfloat16)
    table = jnp.pad(table, (0, TABLE * TILE - table.shape[0])).reshape(1, TABLE, TILE)
    dealt = jnp.concatenate([rows, jnp.broadcast_to(table, (PEERS, TABLE, TILE))], axis=1)
    dealt = lax.all_to_all(dealt, ("y", "c"), 0, 0, tiled=True)
    piece = dealt[:, : NNZ * ROWS]
    table = dealt[:, NNZ * ROWS :].reshape(PEERS, TABLE * TILE).astype(jnp.int32)
    block, live = table[:, :TB], table[:, TB * (1 + NNZ)]
    slot = table[:, TB : TB * (1 + NNZ)].reshape(PEERS, NNZ, TB)
    dead = jnp.arange(TB, dtype=jnp.int32)[None, None, :] >= live[:, None, None]
    slot = jnp.where(dead, SLOTS, slot).reshape(-1)
    x_at = ring_place((x - block // (2 * NZ)) % NX, NX)
    z_at = ring_place((z - (block // 2) % NZ) % NZ, NZ)
    source = jnp.arange(PEERS, dtype=jnp.int32)[:, None] // 2 * 2 + block % 2
    low = jnp.where(x_at == 3, 5, x_at)
    high = jnp.where(x_at == 0, 7, jnp.where(x_at == 3, 6, x_at + 2))
    group = jnp.where(core == 0, z_at, jnp.where(z_at < NX, low, high))
    within = jnp.where(core == 0, x_at, z_at % NX)
    place = ((group * NX + within) * PEERS + source).reshape(-1)
    me = jnp.stack([y, core]).astype(jnp.int32)
    pieces, blocks = gather(piece, after(b_tiles[0], dealt), core)
    packed = accumulate(pieces, blocks, (place, slot, live, me))
    return inflate(lax.all_to_all(packed, ("y", "c"), 0, 0, tiled=True))


def solution(mesh):
    fine = Mesh(mesh.devices.reshape(NY, NX, NZ, 2), ("y", "x", "z", "c"))
    col = ("x", "z", "c")
    in_specs = (
        P(("y",) + col, None, None, None),
        P("y", col, None, None),
        P("y", col),
        P("y", col, None),
        P("y", col),
    )
    out_specs = P("y", col, None, None)
    return jax.shard_map(
        per_device, mesh=fine, in_specs=in_specs, out_specs=out_specs, check_vma=False
    )
```

```python
import functools

import jax
import jax.numpy as jnp
from jax import lax
from jax.experimental import pallas as pl
from jax.experimental.pallas import tpu as pltpu
from jax.sharding import Mesh
from jax.sharding import PartitionSpec as P

JB_DEV = 8
OUT_J = 16
TILE = 128
NNZ = 8
TB = 64
SLOTS = 128
NX, NY, NZ = 4, 4, 8
SIZES = {"y": NY, "x": NX, "z": NZ, "c": 2}
PEERS = 2 * NY
ROWS = TILE // PEERS
SHARE = SLOTS // NY
BODY = SHARE * ROWS
TABLE = 16
UNROLL = 16
MIB = 1024 * 1024
KEPT = pltpu.HBM


def shift(value, axis, step):
    n = SIZES[axis]
    return lax.ppermute(value, axis, [(i, (i + step) % n) for i in range(n)])


def ring_place(distance, n):
    return jnp.maximum(jnp.minimum(2 * distance - 1, 2 * (n - distance)), 0)


def after(value, *others):
    return lax.optimization_barrier((value, *others))[0]


def rise_and_fall(value):
    pairs = []
    for y in range(NY):
        pairs.append((2 * y, 2 * ((y + 1) % NY)))
        pairs.append((2 * y + 1, 2 * ((y - 1) % NY) + 1))
    return lax.ppermute(value, ("y", "c"), pairs)


def cross(value, step0, step1):
    pairs = []
    for x in range(NX):
        for z in range(NZ):
            for core, step in ((0, step0), (1, step1)):
                if step is not None:
                    target = ((x + step[0]) % NX * NZ + (z + step[1]) % NZ) * 2 + core
                    pairs.append(((x * NZ + z) * 2 + core, target))
    return lax.ppermute(value, ("x", "z", "c"), pairs)


def gather(piece, block, core):
    on_x = core == 0
    p1, n1 = cross(piece, (1, 0), (0, 1)), cross(piece, (-1, 0), (0, -1))
    ring1 = rise_and_fall(block)
    swap0 = shift(block, "c", 1)
    p2 = cross(jnp.where(on_x, piece, p1), (2, 0), (0, 1))
    n2 = cross(after(n1, swap0), None, (0, -1))
    base = jnp.concatenate([piece, p1, n1, p2])
    q1, m1 = cross(base, (0, 1), (1, 0)), cross(base, (0, -1), (-1, 0))
    p3, n3 = cross(p2, None, (0, 1)), cross(n2, None, (0, -1))
    ring2 = rise_and_fall(after(ring1, p3))
    p4 = cross(p3, None, (0, 1))
    rest = jnp.concatenate([n2, p3, n3, p4])
    q2 = cross(jnp.where(on_x, q1, rest), (0, 1), (1, 0))
    m2 = cross(jnp.where(on_x, m1, rest), (0, -1), (-1, 0))
    swap1 = shift(after(ring1, q1, m1), "c", 1)
    q3 = cross(jnp.where(on_x, q2, q1), (0, 1), (1, 0))
    m3 = cross(after(m2, swap1), (0, -1), (-1, 0))
    half = q2.shape[0] // 2
    q4 = cross(q2[:half], (0, 2), None)
    m4 = cross(m2[half:], (0, -2), None)
    ring3 = rise_and_fall(after(ring2, m2))
    swap2 = shift(after(ring2, q3, m3), "c", 1)
    swap3 = shift(after(ring3, q4, m4), "c", 1)
    blocks = [block, swap0, ring1, swap1, ring2, swap2, ring3, swap3]
    return [base, q1, m1, q2, m2, q3, m3, q4, m4, rest], blocks


def accumulate_kernel(place, slot, live, me, *refs):
    group = NX * PEERS
    pieces, blocks, out = refs[:10], refs[10 : 10 + PEERS], refs[10 + PEERS]
    left, right, acc0, acc1, odd0, odd1, packed, sems, right_sems, out_sems = refs[11 + PEERS :]
    row, core = me[0], me[1]
    targets = [left.at[pl.ds(n * group, group)] for n in range(7)]
    targets += [left.at[pl.ds(7 * group + n * group // 2, group // 2)] for n in range(2)]
    targets += [left.at[pl.ds(7 * group, group)]]
    copies = [
        pltpu.make_async_copy(piece, target, sems.at[n])
        for n, (piece, target) in enumerate(zip(pieces, targets))
    ]
    right_copies = [
        pltpu.make_async_copy(block, right.at[n], right_sems.at[n])
        for n, block in enumerate(blocks)
    ]
    for copy in right_copies[:2] + copies[:7]:
        copy.start()
    for which, copy in ((0, copies[7]), (0, copies[8]), (1, copies[9])):
        pl.when(core == which)(copy.start)

    def clear(i, carry):
        acc0[i] = jnp.zeros((ROWS, TILE), jnp.float32)
        acc1[i] = jnp.zeros((ROWS, TILE), jnp.float32)
        odd0[i] = jnp.zeros((ROWS, TILE), jnp.float32)
        odd1[i] = jnp.zeros((ROWS, TILE), jnp.float32)
        return carry

    lax.fori_loop(0, SLOTS, clear, 0, unroll=8)
    for copy in copies[:7]:
        copy.wait()
    for which, copy in ((0, copies[7]), (0, copies[8]), (1, copies[9])):
        pl.when(core == which)(copy.wait)
    def multiply(n, source, t):
        return jnp.dot(
            left[place[source * TB + t]], right[n, t], preferred_element_type=jnp.float32
        )

    def steps(panels, first, last):
        def step(s, carry):
            slots = [UNROLL * s + u for u in range(UNROLL)]
            products = [[multiply(n, source, t) for n, source, _ in panels] for t in slots]
            for u in range(0, UNROLL, 2):
                for m in range(NNZ):
                    for parity in range(2):
                        for (_, source, accs), value in zip(panels, products[u + parity]):
                            at = slot[(source * NNZ + m) * TB + slots[u + parity]]
                            accs[parity][at] += value[m * ROWS : (m + 1) * ROWS]
            return carry

        lax.fori_loop(first, last, step, 0)

    for hop in range(NY):
        down, up = lax.rem(row + NY - hop, NY), lax.rem(row + hop, NY)
        own = 2 * jnp.where(core == 0, down, up) + core
        sib = 2 * jnp.where(core == 0, up, down) + 1 - core
        right_copies[2 * hop].wait()
        right_copies[2 * hop + 1].wait()
        if hop + 1 < NY:
            right_copies[2 * hop + 2].start()
            right_copies[2 * hop + 3].start()
        own_panel, sib_panel = (2 * hop, own, (acc0, odd0)), (2 * hop + 1, sib, (acc1, odd1))
        own_steps = (live[own] + UNROLL - 1) // UNROLL
        sib_steps = (live[sib] + UNROLL - 1) // UNROLL
        shared = jnp.minimum(own_steps, sib_steps)
        steps((own_panel, sib_panel), 0, shared)
        steps((own_panel,), shared, own_steps)
        steps((sib_panel,), shared, sib_steps)

    copies = []
    for q, acc, odd in ((0, acc0, odd0), (1, acc1, odd1)):
        totals = [jnp.zeros((8, TILE), jnp.float32)] * JB_DEV
        for y in range(NY):

            def narrow(k, totals, q=q, y=y, acc=acc, odd=odd):
                totals = list(totals)
                for j in range(JB_DEV):
                    value = acc[y * SHARE + k * JB_DEV + j] + odd[y * SHARE + k * JB_DEV + j]
                    value = value * value
                    at = pl.multiple_of((k * JB_DEV + j) * ROWS, ROWS)
                    packed[q, y, pl.ds(at, ROWS)] = value.astype(jnp.bfloat16)
                    totals[j] = totals[j] + value[:8] + value[8:]
                return tuple(totals)

            totals = lax.fori_loop(0, SHARE // JB_DEV, narrow, tuple(totals))
        total = jnp.concatenate(
            [jnp.sum(value, axis=0, keepdims=True) for value in totals], axis=0
        )
        high = total.astype(jnp.bfloat16)
        low = (total - high.astype(jnp.float32)).astype(jnp.bfloat16)
        for y in range(NY):
            packed[q, y, pl.ds(BODY, JB_DEV)] = high
            packed[q, y, pl.ds(BODY + JB_DEV, JB_DEV)] = low
            copy = pltpu.make_async_copy(
                packed.at[q, y], out.at[2 * y + jnp.bitwise_xor(core, q)], out_sems.at[q, y]
            )
            copy.start()
            copies.append(copy)
    for copy in copies:
        copy.wait()


def accumulate(pieces, blocks, tables):
    kept = pl.BlockSpec(memory_space=KEPT)
    grid_spec = pltpu.PrefetchScalarGridSpec(
        num_scalar_prefetch=4,
        grid=(),
        in_specs=[kept] * (len(pieces) + len(blocks)),
        out_specs=pl.BlockSpec(memory_space=pl.ANY),
        scratch_shapes=[
            pltpu.VMEM((NX * NZ * PEERS, NNZ * ROWS, TILE), jnp.bfloat16),
            pltpu.VMEM((PEERS, TB, TILE, TILE), jnp.bfloat16),
            *[pltpu.VMEM((SLOTS + 1, ROWS, TILE), jnp.float32)] * 4,
            pltpu.VMEM((2, NY, BODY + 2 * JB_DEV, TILE), jnp.bfloat16),
            pltpu.SemaphoreType.DMA((len(pieces),)),
            pltpu.SemaphoreType.DMA((PEERS,)),
            pltpu.SemaphoreType.DMA((2, NY)),
        ],
    )
    return pl.pallas_call(
        accumulate_kernel,
        out_shape=jax.ShapeDtypeStruct((PEERS, BODY + 2 * JB_DEV, TILE), jnp.bfloat16),
        grid_spec=grid_spec,
        compiler_params=pltpu.CompilerParams(vmem_limit_bytes=60 * MIB),
        name="accumulate",
    )(*tables, *pieces, *blocks)


def inflate_kernel(source, out):
    total = jnp.zeros((JB_DEV, TILE), jnp.float32)
    for peer in range(PEERS):
        total += source[peer, BODY : BODY + JB_DEV].astype(jnp.float32)
        total += source[peer, BODY + JB_DEV : BODY + 2 * JB_DEV].astype(jnp.float32)
    factor = (OUT_J * TILE) / total
    for j in range(JB_DEV):
        scale = factor[j : j + 1]
        for k in range(SHARE // JB_DEV):
            i = k * JB_DEV + j
            for peer in range(PEERS):
                value = source[peer, i * ROWS : (i + 1) * ROWS].astype(jnp.float32)
                out[i, 0, peer * ROWS : (peer + 1) * ROWS] = (value * scale).astype(jnp.bfloat16)


def inflate(source):
    return pl.pallas_call(
        inflate_kernel,
        out_shape=jax.ShapeDtypeStruct((SHARE, 1, TILE, TILE), jnp.bfloat16),
        in_specs=[pl.BlockSpec(memory_space=pltpu.VMEM)],
        out_specs=pl.BlockSpec(memory_space=pltpu.VMEM),
        compiler_params=pltpu.CompilerParams(vmem_limit_bytes=12 * MIB),
        name="inflate",
    )(source)


def per_device(a_tiles, b_tiles, b_block, c_slot, b_live):
    y, x, z, core = (lax.axis_index(axis) for axis in ("y", "x", "z", "c"))
    rows = a_tiles.reshape(NNZ, PEERS, ROWS, TILE).transpose(1, 0, 2, 3)
    rows = rows.reshape(PEERS, NNZ * ROWS, TILE)
    table = jnp.concatenate(
        [b_block[0], c_slot[0].T.reshape(-1), jnp.broadcast_to(b_live[0], (TB,))]
    ).astype(jnp.bfloat16)
    table = jnp.pad(table, (0, TABLE * TILE - table.shape[0])).reshape(1, TABLE, TILE)
    dealt = jnp.concatenate([rows, jnp.broadcast_to(table, (PEERS, TABLE, TILE))], axis=1)
    dealt = lax.all_to_all(dealt, ("y", "c"), 0, 0, tiled=True)
    piece = dealt[:, : NNZ * ROWS]
    table = dealt[:, NNZ * ROWS :].reshape(PEERS, TABLE * TILE).astype(jnp.int32)
    block, live = table[:, :TB], table[:, TB * (1 + NNZ)]
    slot = table[:, TB : TB * (1 + NNZ)].reshape(PEERS, NNZ, TB)
    dead = jnp.arange(TB, dtype=jnp.int32)[None, None, :] >= live[:, None, None]
    slot = jnp.where(dead, SLOTS, slot).reshape(-1)
    x_at = ring_place((x - block // (2 * NZ)) % NX, NX)
    z_at = ring_place((z - (block // 2) % NZ) % NZ, NZ)
    source = jnp.arange(PEERS, dtype=jnp.int32)[:, None] // 2 * 2 + block % 2
    low = jnp.where(x_at == 3, 5, x_at)
    high = jnp.where(x_at == 0, 7, jnp.where(x_at == 3, 6, x_at + 2))
    group = jnp.where(core == 0, z_at, jnp.where(z_at < NX, low, high))
    within = jnp.where(core == 0, x_at, z_at % NX)
    place = ((group * NX + within) * PEERS + source).reshape(-1)
    me = jnp.stack([y, core]).astype(jnp.int32)
    pieces, blocks = gather(piece, after(b_tiles[0], dealt), core)
    packed = accumulate(pieces, blocks, (place, slot, live, me))
    return inflate(lax.all_to_all(packed, ("y", "c"), 0, 0, tiled=True))


def solution(mesh):
    fine = Mesh(mesh.devices.reshape(NY, NX, NZ, 2), ("y", "x", "z", "c"))
    col = ("x", "z", "c")
    in_specs = (
        P(("y",) + col, None, None, None),
        P("y", col, None, None),
        P("y", col),
        P("y", col, None),
        P("y", col),
    )
    out_specs = P("y", col, None, None)
    return jax.shard_map(
        per_device, mesh=fine, in_specs=in_specs, out_specs=out_specs, check_vma=False
    )
```

```python
import functools

import jax
import jax.numpy as jnp
from jax import lax
from jax.experimental import pallas as pl
from jax.experimental.pallas import tpu as pltpu
from jax.sharding import Mesh
from jax.sharding import PartitionSpec as P

JB_DEV = 8
OUT_J = 16
TILE = 128
NNZ = 8
TB = 64
SLOTS = 128
NX, NY, NZ = 4, 4, 8
SIZES = {"y": NY, "x": NX, "z": NZ, "c": 2}
PEERS = 2 * NY
ROWS = TILE // PEERS
SHARE = SLOTS // NY
BODY = SHARE * ROWS
TABLE = 16
UNROLL = 16
MIB = 1024 * 1024
KEPT = pltpu.HBM


def shift(value, axis, step):
    n = SIZES[axis]
    return lax.ppermute(value, axis, [(i, (i + step) % n) for i in range(n)])


def ring_place(distance, n):
    return jnp.maximum(jnp.minimum(2 * distance - 1, 2 * (n - distance)), 0)


def after(value, *others):
    return lax.optimization_barrier((value, *others))[0]


def rise_and_fall(value):
    pairs = []
    for y in range(NY):
        pairs.append((2 * y, 2 * ((y + 1) % NY)))
        pairs.append((2 * y + 1, 2 * ((y - 1) % NY) + 1))
    return lax.ppermute(value, ("y", "c"), pairs)


def cross(value, step0, step1):
    pairs = []
    for x in range(NX):
        for z in range(NZ):
            for core, step in ((0, step0), (1, step1)):
                if step is not None:
                    target = ((x + step[0]) % NX * NZ + (z + step[1]) % NZ) * 2 + core
                    pairs.append(((x * NZ + z) * 2 + core, target))
    return lax.ppermute(value, ("x", "z", "c"), pairs)


def gather(piece, block, core):
    on_x = core == 0
    p1, n1 = cross(piece, (1, 0), (0, 1)), cross(piece, (-1, 0), (0, -1))
    ring1 = rise_and_fall(block)
    swap0 = shift(block, "c", 1)
    p2 = cross(jnp.where(on_x, piece, p1), (2, 0), (0, 1))
    n2 = cross(after(n1, swap0), None, (0, -1))
    base = jnp.concatenate([piece, p1, n1, p2])
    q1, m1 = cross(base, (0, 1), (1, 0)), cross(base, (0, -1), (-1, 0))
    p3, n3 = cross(p2, None, (0, 1)), cross(n2, None, (0, -1))
    ring2 = rise_and_fall(after(ring1, p3))
    p4 = cross(p3, None, (0, 1))
    rest = jnp.concatenate([n2, p3, n3, p4])
    q2 = cross(jnp.where(on_x, q1, rest), (0, 1), (1, 0))
    m2 = cross(jnp.where(on_x, m1, rest), (0, -1), (-1, 0))
    swap1 = shift(after(ring1, q1, m1), "c", 1)
    q3 = cross(jnp.where(on_x, q2, q1), (0, 1), (1, 0))
    m3 = cross(after(m2, swap1), (0, -1), (-1, 0))
    half = q2.shape[0] // 2
    q4 = cross(q2[:half], (0, 2), None)
    m4 = cross(m2[half:], (0, -2), None)
    ring3 = rise_and_fall(after(ring2, m2))
    swap2 = shift(after(ring2, q3, m3), "c", 1)
    swap3 = shift(after(ring3, q4), "c", 1)
    blocks = [block, swap0, ring1, swap1, ring2, swap2, ring3, swap3]
    return [base, q1, m1, q2, m2, q3, m3, q4, m4, rest], blocks


def accumulate_kernel(place, slot, live, me, *refs):
    group = NX * PEERS
    pieces, blocks, out = refs[:10], refs[10 : 10 + PEERS], refs[10 + PEERS]
    left, right, acc0, acc1, odd0, odd1, packed, sems, right_sems, out_sems = refs[11 + PEERS :]
    row, core = me[0], me[1]
    targets = [left.at[pl.ds(n * group, group)] for n in range(7)]
    targets += [left.at[pl.ds(7 * group + n * group // 2, group // 2)] for n in range(2)]
    targets += [left.at[pl.ds(7 * group, group)]]
    copies = [
        pltpu.make_async_copy(piece, target, sems.at[n])
        for n, (piece, target) in enumerate(zip(pieces, targets))
    ]
    right_copies = [
        pltpu.make_async_copy(block, right.at[n], right_sems.at[n])
        for n, block in enumerate(blocks)
    ]
    for copy in right_copies[:2] + copies[:7]:
        copy.start()
    for which, copy in ((0, copies[7]), (0, copies[8]), (1, copies[9])):
        pl.when(core == which)(copy.start)

    def clear(i, carry):
        acc0[i] = jnp.zeros((ROWS, TILE), jnp.float32)
        acc1[i] = jnp.zeros((ROWS, TILE), jnp.float32)
        odd0[i] = jnp.zeros((ROWS, TILE), jnp.float32)
        odd1[i] = jnp.zeros((ROWS, TILE), jnp.float32)
        return carry

    lax.fori_loop(0, SLOTS, clear, 0, unroll=8)
    for copy in copies[:7]:
        copy.wait()
    for which, copy in ((0, copies[7]), (0, copies[8]), (1, copies[9])):
        pl.when(core == which)(copy.wait)
    def multiply(n, source, t):
        return jnp.dot(
            left[place[source * TB + t]], right[n, t], preferred_element_type=jnp.float32
        )

    def steps(panels, first, last):
        def step(s, carry):
            slots = [UNROLL * s + u for u in range(UNROLL)]
            products = [[multiply(n, source, t) for n, source, _ in panels] for t in slots]
            for u in range(0, UNROLL, 2):
                for m in range(NNZ):
                    for parity in range(2):
                        for (_, source, accs), value in zip(panels, products[u + parity]):
                            at = slot[(source * NNZ + m) * TB + slots[u + parity]]
                            accs[parity][at] += value[m * ROWS : (m + 1) * ROWS]
            return carry

        lax.fori_loop(first, last, step, 0)

    for hop in range(NY):
        down, up = lax.rem(row + NY - hop, NY), lax.rem(row + hop, NY)
        own = 2 * jnp.where(core == 0, down, up) + core
        sib = 2 * jnp.where(core == 0, up, down) + 1 - core
        right_copies[2 * hop].wait()
        right_copies[2 * hop + 1].wait()
        if hop + 1 < NY:
            right_copies[2 * hop + 2].start()
            right_copies[2 * hop + 3].start()
        own_panel, sib_panel = (2 * hop, own, (acc0, odd0)), (2 * hop + 1, sib, (acc1, odd1))
        own_steps = (live[own] + UNROLL - 1) // UNROLL
        sib_steps = (live[sib] + UNROLL - 1) // UNROLL
        shared = jnp.minimum(own_steps, sib_steps)
        steps((own_panel, sib_panel), 0, shared)
        steps((own_panel,), shared, own_steps)
        steps((sib_panel,), shared, sib_steps)

    copies = []
    for q, acc, odd in ((0, acc0, odd0), (1, acc1, odd1)):
        totals = [jnp.zeros((8, TILE), jnp.float32)] * JB_DEV
        for y in range(NY):

            def narrow(k, totals, q=q, y=y, acc=acc, odd=odd):
                totals = list(totals)
                for j in range(JB_DEV):
                    value = acc[y * SHARE + k * JB_DEV + j] + odd[y * SHARE + k * JB_DEV + j]
                    value = value * value
                    at = pl.multiple_of((k * JB_DEV + j) * ROWS, ROWS)
                    packed[q, y, pl.ds(at, ROWS)] = value.astype(jnp.bfloat16)
                    totals[j] = totals[j] + value[:8] + value[8:]
                return tuple(totals)

            totals = lax.fori_loop(0, SHARE // JB_DEV, narrow, tuple(totals))
        total = jnp.concatenate(
            [jnp.sum(value, axis=0, keepdims=True) for value in totals], axis=0
        )
        high = total.astype(jnp.bfloat16)
        low = (total - high.astype(jnp.float32)).astype(jnp.bfloat16)
        for y in range(NY):
            packed[q, y, pl.ds(BODY, JB_DEV)] = high
            packed[q, y, pl.ds(BODY + JB_DEV, JB_DEV)] = low
            copy = pltpu.make_async_copy(
                packed.at[q, y], out.at[2 * y + jnp.bitwise_xor(core, q)], out_sems.at[q, y]
            )
            copy.start()
            copies.append(copy)
    for copy in copies:
        copy.wait()


def accumulate(pieces, blocks, tables):
    kept = pl.BlockSpec(memory_space=KEPT)
    grid_spec = pltpu.PrefetchScalarGridSpec(
        num_scalar_prefetch=4,
        grid=(),
        in_specs=[kept] * (len(pieces) + len(blocks)),
        out_specs=pl.BlockSpec(memory_space=pl.ANY),
        scratch_shapes=[
            pltpu.VMEM((NX * NZ * PEERS, NNZ * ROWS, TILE), jnp.bfloat16),
            pltpu.VMEM((PEERS, TB, TILE, TILE), jnp.bfloat16),
            *[pltpu.VMEM((SLOTS + 1, ROWS, TILE), jnp.float32)] * 4,
            pltpu.VMEM((2, NY, BODY + 2 * JB_DEV, TILE), jnp.bfloat16),
            pltpu.SemaphoreType.DMA((len(pieces),)),
            pltpu.SemaphoreType.DMA((PEERS,)),
            pltpu.SemaphoreType.DMA((2, NY)),
        ],
    )
    return pl.pallas_call(
        accumulate_kernel,
        out_shape=jax.ShapeDtypeStruct((PEERS, BODY + 2 * JB_DEV, TILE), jnp.bfloat16),
        grid_spec=grid_spec,
        compiler_params=pltpu.CompilerParams(vmem_limit_bytes=60 * MIB),
        name="accumulate",
    )(*tables, *pieces, *blocks)


def inflate_kernel(source, out):
    total = jnp.zeros((JB_DEV, TILE), jnp.float32)
    for peer in range(PEERS):
        total += source[peer, BODY : BODY + JB_DEV].astype(jnp.float32)
        total += source[peer, BODY + JB_DEV : BODY + 2 * JB_DEV].astype(jnp.float32)
    factor = (OUT_J * TILE) / total
    for j in range(JB_DEV):
        scale = factor[j : j + 1]
        for k in range(SHARE // JB_DEV):
            i = k * JB_DEV + j
            for peer in range(PEERS):
                value = source[peer, i * ROWS : (i + 1) * ROWS].astype(jnp.float32)
                out[i, 0, peer * ROWS : (peer + 1) * ROWS] = (value * scale).astype(jnp.bfloat16)


def inflate(source):
    return pl.pallas_call(
        inflate_kernel,
        out_shape=jax.ShapeDtypeStruct((SHARE, 1, TILE, TILE), jnp.bfloat16),
        in_specs=[pl.BlockSpec(memory_space=pltpu.VMEM)],
        out_specs=pl.BlockSpec(memory_space=pltpu.VMEM),
        compiler_params=pltpu.CompilerParams(vmem_limit_bytes=12 * MIB),
        name="inflate",
    )(source)


def per_device(a_tiles, b_tiles, b_block, c_slot, b_live):
    y, x, z, core = (lax.axis_index(axis) for axis in ("y", "x", "z", "c"))
    rows = a_tiles.reshape(NNZ, PEERS, ROWS, TILE).transpose(1, 0, 2, 3)
    rows = rows.reshape(PEERS, NNZ * ROWS, TILE)
    table = jnp.concatenate(
        [b_block[0], c_slot[0].T.reshape(-1), jnp.broadcast_to(b_live[0], (TB,))]
    ).astype(jnp.bfloat16)
    table = jnp.pad(table, (0, TABLE * TILE - table.shape[0])).reshape(1, TABLE, TILE)
    dealt = jnp.concatenate([rows, jnp.broadcast_to(table, (PEERS, TABLE, TILE))], axis=1)
    dealt = lax.all_to_all(dealt, ("y", "c"), 0, 0, tiled=True)
    piece = dealt[:, : NNZ * ROWS]
    table = dealt[:, NNZ * ROWS :].reshape(PEERS, TABLE * TILE).astype(jnp.int32)
    block, live = table[:, :TB], table[:, TB * (1 + NNZ)]
    slot = table[:, TB : TB * (1 + NNZ)].reshape(PEERS, NNZ, TB)
    dead = jnp.arange(TB, dtype=jnp.int32)[None, None, :] >= live[:, None, None]
    slot = jnp.where(dead, SLOTS, slot).reshape(-1)
    x_at = ring_place((x - block // (2 * NZ)) % NX, NX)
    z_at = ring_place((z - (block // 2) % NZ) % NZ, NZ)
    source = jnp.arange(PEERS, dtype=jnp.int32)[:, None] // 2 * 2 + block % 2
    low = jnp.where(x_at == 3, 5, x_at)
    high = jnp.where(x_at == 0, 7, jnp.where(x_at == 3, 6, x_at + 2))
    group = jnp.where(core == 0, z_at, jnp.where(z_at < NX, low, high))
    within = jnp.where(core == 0, x_at, z_at % NX)
    place = ((group * NX + within) * PEERS + source).reshape(-1)
    me = jnp.stack([y, core]).astype(jnp.int32)
    pieces, blocks = gather(piece, after(b_tiles[0], dealt), core)
    packed = accumulate(pieces, blocks, (place, slot, live, me))
    return inflate(lax.all_to_all(packed, ("y", "c"), 0, 0, tiled=True))


def solution(mesh):
    fine = Mesh(mesh.devices.reshape(NY, NX, NZ, 2), ("y", "x", "z", "c"))
    col = ("x", "z", "c")
    in_specs = (
        P(("y",) + col, None, None, None),
        P("y", col, None, None),
        P("y", col),
        P("y", col, None),
        P("y", col),
    )
    out_specs = P("y", col, None, None)
    return jax.shard_map(
        per_device, mesh=fine, in_specs=in_specs, out_specs=out_specs, check_vma=False
    )
```
